128 devices in a mesh: lon: 16 (over y_hi, z, core), lat: 8 (over x, y_lo).
Axes of the slice: x: 4, y: 4 (y_hi: 2, y_lo: 2; y = y_hi * 2 + y_lo), z: 4, core: 2. Of those that a mesh axis runs over, the one named last changes fastest.
Arguments:
- tracers: float32 [4, 1024, 512, 128], P(None, 'lon', 'lat'), may hold values from 0.2 to 2
- kdiff: float32 [1024, 512, 128], P('lon', 'lat'), may hold values from 0.3 to 8
- photolysis: float32 [1024, 512, 128], P('lon', 'lat'), may hold values from 0.05 to 2
- u_wind: float32 [1024, 512, 128], P('lon', 'lat'), may hold values from -0.24 to 0.24
- v_wind: float32 [1024, 512, 128], P('lon', 'lat'), may hold values from -0.24 to 0.24
- day_count: int32 [16, 8], replicated, may hold values from 0 to 32, as said below
- day_order: int32 [16, 8, 32], P('lon', 'lat'), may hold values from 0 to 31, each once within a row
Outputs:
- tracers_next: float32 [4, 1024, 512, 128], P(None, 'lon', 'lat')
The draws below stay inside these ranges and needn't reach their ends.
Inputs may be any that keep to these rules, and one draw needn't show every extreme that they name: Tile (i, j) has day_count[i, j] daylit blocks, named by the first entries of day_order[i, j, :].
All inputs are finite; a program needn't handle non-finite values.
Results may differ from the reference program's by a relative error of at most 0.00002.
Values sent between devices are 32-bit elements; how exact they have to be, the bound alone decides.
A program may use at most 128 MiB of HBM per device.

```python
import math
import jax
import jax.numpy as jnp
from jax import lax

CLON = 64
CLAT = 64
LEV = 128
SPECIES = 4
BCOL = 128
SECTIONS = 12
TLON = 16
TLAT = 8
NLON = 1024
NLAT = 512
BLK = 32
HALF = 16


def draw_day_count(key, part):
    key_phase = jax.random.fold_in(key, 11)
    key_lit = jax.random.fold_in(key, 23)
    key_dark = jax.random.fold_in(key, 37)
    phase = jax.random.randint(key_phase, (), 0, TLON)
    lon_tiles = jnp.arange(TLON, dtype=jnp.int32)[:, None]
    lat_tiles = jnp.arange(TLAT, dtype=jnp.int32)[None, :]
    row_phase = phase + lat_tiles % 2 * (TLON // 2)
    relative = (lon_tiles - row_phase) % TLON
    dayside = relative < TLON // 2
    lit_counts = jax.random.randint(key_lit, (TLON, TLAT), HALF, BLK + 1)
    dark_counts = jax.random.randint(key_dark, (TLON, TLAT), 0, HALF // 4 + 1)
    counts = jnp.where(dayside, lit_counts, dark_counts)
    counts = jnp.where((relative == 0) & (lat_tiles == 0), BLK, counts)
    counts = jnp.where((relative == TLON // 2) & (lat_tiles == 0), 0, counts)
    return counts.astype(jnp.int32)


def level_of(stream_key, dims, pieces, least, top_value):
    def one(position, shards_of):
        steps = jax.random.uniform(jax.random.fold_in(jax.random.fold_in(stream_key, 6), position), (shards_of,), jnp.float32, least / len(pieces), top_value / len(pieces))
        return jnp.repeat(jnp.exp(steps), dims[position] // shards_of).reshape((-1,) + (1,) * (len(dims) - position - 1))

    level = one(*pieces[0])
    for cut in pieces[1:]:
        level = level * one(*cut)
    return level


def setup_inputs(seed: int = 0) -> dict:
    keys = jax.random.split(jax.random.key(seed), 8)
    return {
        "tracers": jnp.clip(jnp.exp(math.log(2.0) - 2.3025851 * jax.random.uniform(keys[0], (SPECIES, NLON, NLAT, LEV), jnp.float32) ** level_of(keys[0], (SPECIES, NLON, NLAT, LEV), ((1, 16), (2, 8)), -0.2, 0.2)), 0.2, 2.0),
        "kdiff": jnp.clip(jnp.exp(math.log(8.0) - 3.2834143 * jax.random.uniform(keys[1], (NLON, NLAT, LEV), jnp.float32) ** level_of(keys[1], (NLON, NLAT, LEV), ((0, 16), (1, 8)), -0.2, 0.2)), 0.3, 8.0),
        "photolysis": jnp.clip(jnp.exp(math.log(2.0) - 3.6888794 * jax.random.uniform(keys[2], (NLON, NLAT, LEV), jnp.float32) ** level_of(keys[2], (NLON, NLAT, LEV), ((0, 16), (1, 8)), -0.2, 0.2)), 0.05, 2.0),
        "u_wind": jnp.clip(jax.random.uniform(keys[3], (NLON, NLAT, LEV), jnp.float32, -0.24, 0.24) * level_of(keys[3], (NLON, NLAT, LEV), ((0, 16), (1, 8)), -0.4, 0.0), -0.24, 0.24),
        "v_wind": jnp.clip(jax.random.uniform(keys[4], (NLON, NLAT, LEV), jnp.float32, -0.24, 0.24) * level_of(keys[4], (NLON, NLAT, LEV), ((0, 16), (1, 8)), -0.4, 0.0), -0.24, 0.24),
        "day_count": draw_day_count(jax.random.fold_in(keys[7], 71), 0),
        "day_order": jax.vmap(lambda own: jax.random.permutation(own, BLK))(jax.random.split(keys[6], TLON * TLAT)).reshape((TLON, TLAT, BLK)).astype(jnp.int32),
    }


def section_table(sections):
    bvals = [1.0 / 3.0] * 3 + [(j * j + j - 2.0) / (2.0 * j * (j + 1.0)) for j in range(3, sections + 1)]
    scale = 4.0 / (sections * sections + sections - 2.0)
    rows = []
    for j in range(2, sections + 1):
        coef_prev = (2.0 * j - 1.0) / j * bvals[j] / bvals[j - 1]
        coef_back = -(j - 1.0) / j * bvals[j] / bvals[j - 2]
        coef_step = coef_prev * scale
        coef_first = -(1.0 - bvals[j - 1]) * coef_step
        rows.append((coef_prev, coef_back, 1.0 - coef_prev - coef_back, coef_step, coef_first))
    return bvals[1] * scale, rows


def tendency(field, diffusion, photo):
    above = jnp.concatenate([field[..., 1:], field[..., -1:]], axis=-1)
    upward = diffusion * (above - field)
    below = jnp.concatenate([jnp.zeros_like(upward[..., :1]), upward[..., :-1]], axis=-1)
    mixing = upward - below
    ozone, oxygen, nitric, dioxide = field[0], field[1], field[2], field[3]
    titration = ozone * nitric
    split_no2 = 2.0 * photo * dioxide
    split_o3 = 0.25 * photo * ozone
    chemistry = jnp.stack([1.5 * oxygen - titration - split_o3,
                           split_no2 + split_o3 - 1.5 * oxygen,
                           split_no2 - titration,
                           titration - split_no2], axis=0)
    return mixing + 0.5 * chemistry


def column_step(field, diffusion, photo):
    first_coef, table = section_table(SECTIONS)
    start_rate = tendency(field, diffusion, photo)
    previous = field
    current = field + first_coef * start_rate
    for coef_prev, coef_back, coef_base, coef_step, coef_first in table:
        following = (coef_prev * current + coef_back * previous + coef_base * field
                     + coef_step * tendency(current, diffusion, photo) + coef_first * start_rate)
        previous, current = current, following
    return current


def night_step(field):
    ozone, oxygen, nitric = field[0], field[1], field[2]
    titration = ozone * nitric
    change = jnp.stack([1.5 * oxygen - titration, -1.5 * oxygen, -titration, titration], axis=0)
    return field + 0.5 * change


def daylit_columns(day_count, day_order):
    positions = jnp.arange(BLK, dtype=jnp.int32)
    live = positions[None, None, :] < day_count[:, :, None]
    match = day_order[:, :, :, None] == positions[None, None, None, :]
    daylit = jnp.any(match & live[:, :, :, None], axis=2)
    per_column = jnp.repeat(daylit, BCOL, axis=2)
    per_column = per_column.reshape(TLON, TLAT, CLON, CLAT).transpose(0, 2, 1, 3)
    return per_column.reshape(TLON, CLON * NLAT)


def reference(tracers, kdiff, photolysis, u_wind, v_wind, day_count, day_order):
    slabs = jnp.moveaxis(tracers.reshape(SPECIES, TLON, CLON * NLAT, LEV), 1, 0)
    diff_slabs = kdiff.reshape(TLON, CLON * NLAT, LEV)
    photo_slabs = photolysis.reshape(TLON, CLON * NLAT, LEV)
    lit = daylit_columns(day_count, day_order)

    def one_slab(items):
        field, diffusion, photo, mask = items
        return jnp.where(mask[None, :, None], column_step(field, diffusion, photo), night_step(field))

    stepped = lax.map(one_slab, (slabs, diff_slabs, photo_slabs, lit))
    stepped = jnp.moveaxis(stepped, 0, 1).reshape(SPECIES, NLON, NLAT, LEV)

    def advect_one(field):
        east = jnp.maximum(u_wind, 0.0) * field + jnp.minimum(u_wind, 0.0) * jnp.roll(field, -1, axis=0)
        west = jnp.roll(east, 1, axis=0)
        ahead = jnp.concatenate([field[:, 1:], jnp.zeros_like(field[:, :1])], axis=1)
        north = jnp.maximum(v_wind, 0.0) * field + jnp.minimum(v_wind, 0.0) * ahead
        south = jnp.concatenate([jnp.zeros_like(north[:, :1]), north[:, :-1]], axis=1)
        return field - (east - west) - (north - south)

    return lax.map(advect_one, stepped)
```

```python
import functools

import jax
import jax.numpy as jnp
from jax import lax
from jax.experimental import pallas as pl
from jax.experimental.pallas import tpu as pltpu
from jax.sharding import PartitionSpec as P

SECTIONS = 12
LEV = 128
UNROLL = 32
F32 = jnp.float32
ANY = pl.BlockSpec(memory_space=pl.ANY)
SMEM = pl.BlockSpec(memory_space=pltpu.SMEM)


def section_table(sections):
    bvals = [1.0 / 3.0] * 3 + [
        (j * j + j - 2.0) / (2.0 * j * (j + 1.0)) for j in range(3, sections + 1)
    ]
    scale = 4.0 / (sections * sections + sections - 2.0)
    lead = [1.0, 1.0]
    for j in range(2, sections + 1):
        lead.append(lead[-1] * (2.0 * j - 1.0) / j)
    return bvals, scale, lead


BVALS, SCALE, LEAD = section_table(SECTIONS)


def level_rows(level):
    return pl.ds(pl.multiple_of(level * 8, 8), 8)


def stage(j, cur, old, out, first, kdt, pht, tit):
    keep, share, lead = 1.0 - BVALS[j - 1], BVALS[j - 1], LEAD[j - 1]
    shift = keep / (share * lead)
    product = SCALE * share * lead / 2.0
    offset = SCALE * shift / 2.0
    decay = 0.75 * SCALE
    back = (j - 1.0) / j * LEAD[j - 2] / LEAD[j] if j > 1 else 0.0

    def step(i, carry):
        here, below = list(carry[:4]), list(carry[4:])
        for r in range(UNROLL):
            level = i * UNROLL + r
            rows, above_rows = level_rows(level), level_rows(level + 1)
            mixing = kdt[rows, :]
            above = [cur[q, above_rows, :] for q in range(4)]
            upward = [mixing * (above[q] - here[q]) for q in range(4)]
            state = [(here[q] + upward[q]) - below[q] for q in range(4)]
            if j == 1:
                titration = (SCALE / 2.0) * tit[rows, :]
            else:
                titration = (
                    product
                    * (here[0] + shift * first[0, rows, :])
                    * (here[2] + shift * first[2, rows, :])
                    - offset * tit[rows, :]
                )
            split = pht[0, rows, :] * here[3]
            net = split - titration
            joined = decay * here[1] - pht[1, rows, :] * here[0]
            state = [
                state[0] + (joined - titration),
                state[1] + (split - joined),
                state[2] + net,
                state[3] - net,
            ]
            if j > 1:
                state = [state[q] - back * old[q, rows, :] for q in range(4)]
            for q in range(4):
                out[q, rows, :] = state[q]
            here, below = above, upward
        return (*here, *below)

    zero = jnp.zeros((8, LEV), F32)
    init = tuple(cur[q, pl.ds(0, 8), :] for q in range(4)) + (zero,) * 4
    lax.fori_loop(0, LEV // UNROLL, step, init)


def advance_group(y_nat, k_nat, p_nat, row0, work, ready, lit_of, put):
    first, ping, pong, kdt, pht, tit = work
    zero = jnp.zeros((8, LEV), F32)

    def tile_in(tile, carry):
        src = pl.ds(pl.multiple_of(row0 + tile * 128, 8), 128)
        dst = pl.ds(tile, 128, stride=8)
        for q in range(4):
            first[q, dst, :] = y_nat[q, src, :].T
        kdt[dst, :] = (SCALE * k_nat[src, :]).T
        light = (SCALE * p_nat[src, :]).T
        pht[0, dst, :] = light
        pht[1, dst, :] = 0.125 * light
        return carry

    tile = 0
    for count, wait in ready:
        wait()
        lax.fori_loop(tile, tile + count, tile_in, 0)
        tile += count
    kdt[pl.ds(LEV * 8 - 8, 8), :] = zero
    for q in range(4):
        for ref in (first, ping, pong):
            ref[q, pl.ds(LEV * 8, 8), :] = zero

    def products(i, carry):
        for r in range(16):
            rows = level_rows(i * 16 + r)
            tit[rows, :] = first[0, rows, :] * first[2, rows, :]
        return carry

    lax.fori_loop(0, LEV // 16, products, 0)
    cur, old = first, None
    for j in range(1, SECTIONS + 1):
        out = ping if j % 2 else pong
        stage(j, cur, old, out, first, kdt, pht, tit)
        cur, old = out, cur
    keep = 1.0 - BVALS[SECTIONS]
    share = BVALS[SECTIONS] * LEAD[SECTIONS]

    def tile_out(tile, carry):
        dst = pl.ds(tile, 128, stride=8)
        day = [(keep * first[q, dst, :] + share * cur[q, dst, :]).T for q in range(4)]
        for r in range(16):
            octet = tile * 16 + r
            rows = pl.ds(pl.multiple_of(row0 + octet * 8, 8), 8)
            ozone, oxygen, nitric, dioxide = [y_nat[q, rows, :] for q in range(4)]
            half = 0.5 * (ozone * nitric)
            gain = 0.75 * oxygen
            night = [ozone + (gain - half), oxygen - gain, nitric - half, dioxide + half]
            lit = jnp.full((8, LEV), lit_of(octet), jnp.int32) > 0
            put(octet, rows, [jnp.where(lit, day[q][r * 8 : r * 8 + 8], night[q]) for q in range(4)])
        return carry

    lax.fori_loop(0, 8, tile_out, 0)


def fill_lit(lit, count_ref, order_ref):
    count = count_ref[lax.axis_index("lon"), lax.axis_index("lat")]

    def mark(i, carry):
        lit[order_ref[0, 0, i]] = (i < count).astype(jnp.int32)
        return carry

    lax.fori_loop(0, lit.shape[0], mark, 0)


def sixth(n):
    return lax.shift_right_logical(n * 10923, 16)


def inner_longitude(octet):
    place = sixth(octet)
    return jnp.where(place == 0, 0, jnp.where(place == 1, 63, place - 1))


class Copies:
    def __init__(self, sems):
        self.sems, self.used = sems, 0

    def start(self, pairs):
        group = []
        for src, dst in pairs:
            copy = pltpu.make_async_copy(src, dst, self.sems.at[self.used])
            self.used += 1
            copy.start()
            group.append(copy)
        return lambda: [copy.wait() for copy in group]


def flat(ref):
    return ref.reshape(*ref.shape[:-3], ref.shape[-3] * ref.shape[-2], LEV)


def edge_kernel(
    y, k, p, u, v, count, order,
    polar, inner, north_row, south_row, east_row, west_row,
    ty1, tk1, tp1, ty2, tk2, tp2, urow, vrow, lit, *rest,
):
    work, sems = rest[:-1], rest[-1]
    copies = Copies(sems)
    ready = []
    for c in range(4):
        lons = pl.ds(16 * c, 16)
        pairs = []
        for lats, rows in ((pl.ds(0, 8), pl.ds(0, 8)), (pl.ds(56, 8), pl.ds(8, 8))):
            pairs.append((y.at[:, lons, lats], ty1.at[:, lons, rows]))
            pairs.append((k.at[lons, lats], tk1.at[lons, rows]))
            pairs.append((p.at[lons, lats], tp1.at[lons, rows]))
        ready.append((2, copies.start(pairs)))
    lats = pl.ds(8, 48)
    pairs = [(u.at[63], urow), (v.at[:, 63], vrow)]
    for src, dst in ((pl.ds(0, 1), pl.ds(0, 1)), (pl.ds(63, 1), pl.ds(1, 1)), (pl.ds(1, 20), pl.ds(2, 20))):
        pairs.append((y.at[:, src, lats], ty2.at[:, dst]))
        pairs.append((k.at[src, lats], tk2.at[dst]))
        pairs.append((p.at[src, lats], tp2.at[dst]))
    second = copies.start(pairs)
    fill_lit(lit, count, order)

    y1, y2 = flat(ty1), flat(ty2)

    def put1(octet, rows, values):
        for q in range(4):
            y1[q, rows, :] = values[q]

    def put2(octet, rows, values):
        for q in range(4):
            y2[q, rows, :] = values[q]

    advance_group(
        y1, flat(tk1), flat(tp1), 0, work, ready,
        lambda octet: lit[lax.shift_right_logical(octet, 2)], put1,
    )
    second()
    done1 = copies.start([
        (urow, west_row.at[4]),
        (vrow, south_row.at[4]),
        (ty1, polar),
        (ty1.at[:, :, 0], north_row),
        (ty1.at[:, :, 15], south_row.at[pl.ds(0, 4)]),
        (ty1.at[:, 0, pl.ds(0, 8)], east_row.at[:, pl.ds(0, 8)]),
        (ty1.at[:, 0, pl.ds(8, 8)], east_row.at[:, pl.ds(56, 8)]),
        (ty1.at[:, 63, pl.ds(0, 8)], west_row.at[pl.ds(0, 4), pl.ds(0, 8)]),
        (ty1.at[:, 63, pl.ds(8, 8)], west_row.at[pl.ds(0, 4), pl.ds(56, 8)]),
    ])
    advance_group(
        y2, flat(tk2), flat(tp2), 0, work, [(8, lambda: None)],
        lambda octet: lit[lax.shift_right_logical(inner_longitude(octet), 1)], put2,
    )
    done2 = copies.start([
        (ty2, inner),
        (ty2.at[:, 0], east_row.at[:, pl.ds(8, 48)]),
        (ty2.at[:, 1], west_row.at[pl.ds(0, 4), pl.ds(8, 48)]),
    ])
    done1()
    done2()


def load_inner(copies, y, k, p, ty, tk, tp, lon0):
    lats = pl.ds(8, 48)
    ready = []
    for c in range(2):
        src, dst = pl.ds(lon0 + 11 * c, 11), pl.ds(11 * c, 11)
        ready.append((4, copies.start([
            (y.at[:, src, lats], ty.at[:, dst]),
            (k.at[src, lats], tk.at[dst]),
            (p.at[src, lats], tp.at[dst]),
        ])))
    return ready


def middle_kernel(y, k, p, count, order, inner, ty, tk, tp, lit, *rest):
    work, sems = rest[:-1], rest[-1]
    copies = Copies(sems)
    ready = load_inner(copies, y, k, p, ty, tk, tp, 20)
    fill_lit(lit, count, order)
    flat_y = flat(ty)

    def put(octet, rows, values):
        for q in range(4):
            flat_y[q, rows, :] = values[q]

    advance_group(
        flat_y, flat(tk), flat(tp), 16, work, ready,
        lambda octet: lit[lax.shift_right_logical(inner_longitude(octet + 128), 1)], put,
    )
    copies.start([(ty, inner)])()


CHUNK = 4


def last_kernel(
    y, k, p, u, v, count, order, polar, inner1, inner2, own_row, h_north, h_south, h_east, h_west,
    out,
    ty, tk, tp, mixed, uwind, vwind, first_row, s_halo, w_halo, south, eastward, northward, stage_out, lit,
    *rest,
):
    work, out_sems, sems = rest[:-2], rest[-2], rest[-1]
    copies = Copies(sems)
    ready = load_inner(copies, y, k, p, ty, tk, tp, 41)
    fill_lit(lit, count, order)
    body = pl.ds(1, 64)
    lats = pl.ds(16, 48)
    filled = copies.start([
        (u, uwind),
        (v, vwind),
        (own_row, first_row),
        (h_south, s_halo),
        (h_west, w_halo),
        (h_north, mixed.at[:, body, 72]),
        (h_east, mixed.at[:, 65, pl.ds(8, 64)]),
        (polar.at[:, :, pl.ds(0, 8)], mixed.at[:, body, pl.ds(8, 8)]),
        (polar.at[:, :, pl.ds(8, 8)], mixed.at[:, body, pl.ds(64, 8)]),
        (inner1.at[:, 0], mixed.at[:, 1, lats]),
        (inner1.at[:, 1], mixed.at[:, 64, lats]),
        (inner1.at[:, pl.ds(2, 19)], mixed.at[:, pl.ds(2, 19), lats]),
        (inner1.at[:, 21, pl.ds(0, 16)], mixed.at[:, 21, pl.ds(16, 16)]),
        (inner2.at[:, 0, pl.ds(16, 32)], mixed.at[:, 21, pl.ds(32, 32)]),
        (inner2.at[:, pl.ds(1, 20)], mixed.at[:, pl.ds(22, 20), lats]),
        (inner2.at[:, 21, pl.ds(0, 32)], mixed.at[:, 42, pl.ds(16, 32)]),
    ])

    def put(octet, rows, values):
        place = sixth(octet + 256)
        part = octet + 256 - 6 * place
        dst = pl.ds(pl.multiple_of(part * 8 + 16, 8), 8)
        for q in range(4):
            mixed[q, place, dst, :] = values[q]

    advance_group(
        flat(ty), flat(tk), flat(tp), 32, work, ready,
        lambda octet: lit[lax.shift_right_logical(sixth(octet + 256) - 1, 1)], put,
    )
    filled()
    for m in range(8):
        rows = pl.ds(8 * m, 8)
        wind, gust = w_halo[4, rows, :], s_halo[4, rows, :]
        for q in range(4):
            eastward[q, rows, :] = wind * jnp.where(
                wind > 0, w_halo[q, rows, :], mixed[q, 1, pl.ds(8 + 8 * m, 8), :]
            )
            south[q, rows, :] = gust * jnp.where(gust > 0, s_halo[q, rows, :], first_row[q, rows, :])

    def out_copy(chunk, slot):
        return pltpu.make_async_copy(
            stage_out.at[slot], out.at[:, pl.ds(chunk * CHUNK, CHUNK)], out_sems.at[slot]
        )

    def chunk_step(chunk, carry):
        slot = lax.rem(chunk, 2)

        @pl.when(chunk >= 2)
        def _():
            out_copy(chunk - 2, slot).wait()

        def lon_step(local, inner_carry):
            lon = chunk * CHUNK + local
            for q in range(4):
                northward[q, pl.ds(7, 1), :] = south[q, pl.ds(lon, 1), :]
            for m in range(8):
                rows = pl.ds(8 * m, 8)
                here_rows = pl.ds(8 + 8 * m, 8)
                wind, gust = uwind[lon, rows, :], vwind[lon, rows, :]
                wind_up, gust_up = wind > 0, gust > 0
                for q in range(4):
                    here = mixed[q, lon + 1, here_rows, :]
                    east = wind * jnp.where(wind_up, here, mixed[q, lon + 2, here_rows, :])
                    north = gust * jnp.where(gust_up, here, mixed[q, lon + 1, pl.ds(9 + 8 * m, 8), :])
                    west = eastward[q, rows, :]
                    eastward[q, rows, :] = east
                    northward[q, here_rows, :] = north
                    below = northward[q, pl.ds(7 + 8 * m, 8), :]
                    stage_out[slot, q, local, rows, :] = here - (east - west) - (north - below)
            return inner_carry

        lax.fori_loop(0, CHUNK, lon_step, 0)
        out_copy(chunk, slot).start()
        return carry

    chunks = 64 // CHUNK
    lax.fori_loop(0, chunks, chunk_step, 0)
    for chunk in (chunks - 2, chunks - 1):
        out_copy(chunk, chunk % 2).wait()


WORK = [
    pltpu.VMEM((4, LEV * 8 + 8, LEV), F32),
    pltpu.VMEM((4, LEV * 8 + 8, LEV), F32),
    pltpu.VMEM((4, LEV * 8 + 8, LEV), F32),
    pltpu.VMEM((LEV * 8, LEV), F32),
    pltpu.VMEM((2, LEV * 8, LEV), F32),
    pltpu.VMEM((LEV * 8, LEV), F32),
]
INNER = [
    pltpu.VMEM((4, 22, 48, LEV), F32),
    pltpu.VMEM((22, 48, LEV), F32),
    pltpu.VMEM((22, 48, LEV), F32),
]
LIT = pltpu.SMEM((32,), jnp.int32)


def shape(*dims):
    return jax.ShapeDtypeStruct(dims, F32)


def cost(groups):
    return pl.CostEstimate(
        flops=groups * 128 * 1024 * 540, bytes_accessed=groups * 5 * 2**20, transcendentals=0
    )


PARAMS = pltpu.CompilerParams(vmem_limit_bytes=60 * 2**20)


def body(tracers, kdiff, photolysis, u_wind, v_wind, day_count, day_order):
    polar, inner1, north_row, south_row, east_row, west_row = pl.pallas_call(
        edge_kernel,
        name="edge_groups",
        out_shape=(
            shape(4, 64, 16, LEV), shape(4, 22, 48, LEV),
            shape(4, 64, LEV), shape(5, 64, LEV), shape(4, 64, LEV), shape(5, 64, LEV),
        ),
        in_specs=[ANY] * 5 + [SMEM] * 2,
        out_specs=(ANY,) * 6,
        scratch_shapes=[
            pltpu.VMEM((4, 64, 16, LEV), F32),
            pltpu.VMEM((64, 16, LEV), F32),
            pltpu.VMEM((64, 16, LEV), F32),
            *INNER,
            pltpu.VMEM((64, LEV), F32),
            pltpu.VMEM((64, LEV), F32),
            LIT, *WORK, pltpu.SemaphoreType.DMA((48,)),
        ],
        compiler_params=PARAMS,
        cost_estimate=cost(2),
    )(tracers, kdiff, photolysis, u_wind, v_wind, day_count, day_order)

    lats, lons = lax.axis_size("lat"), lax.axis_size("lon")
    h_north = lax.ppermute(north_row, "lat", [(i + 1, i) for i in range(lats - 1)])
    h_south = lax.ppermute(south_row, "lat", [(i, i + 1) for i in range(lats - 1)])
    h_east = lax.ppermute(east_row, "lon", [((i + 1) % lons, i) for i in range(lons)])
    h_west = lax.ppermute(west_row, "lon", [(i, (i + 1) % lons) for i in range(lons)])

    inner2 = pl.pallas_call(
        middle_kernel,
        name="middle_group",
        out_shape=shape(4, 22, 48, LEV),
        in_specs=[ANY] * 3 + [SMEM] * 2,
        out_specs=ANY,
        scratch_shapes=[*INNER, LIT, *WORK, pltpu.SemaphoreType.DMA((8,))],
        compiler_params=PARAMS,
        cost_estimate=cost(1),
    )(tracers, kdiff, photolysis, day_count, day_order)

    return pl.pallas_call(
        last_kernel,
        name="last_group",
        out_shape=shape(4, 64, 64, LEV),
        in_specs=[ANY] * 5 + [SMEM] * 2 + [ANY] * 8,
        out_specs=ANY,
        scratch_shapes=[
            *INNER,
            pltpu.VMEM((4, 66, 80, LEV), F32),
            pltpu.VMEM((64, 64, LEV), F32),
            pltpu.VMEM((64, 64, LEV), F32),
            pltpu.VMEM((4, 64, LEV), F32),
            pltpu.VMEM((5, 64, LEV), F32),
            pltpu.VMEM((5, 64, LEV), F32),
            pltpu.VMEM((4, 64, LEV), F32),
            pltpu.VMEM((4, 64, LEV), F32),
            pltpu.VMEM((4, 72, LEV), F32),
            pltpu.VMEM((2, 4, CHUNK, 64, LEV), F32),
            LIT, *WORK, pltpu.SemaphoreType.DMA((2,)), pltpu.SemaphoreType.DMA((24,)),
        ],
        compiler_params=PARAMS,
        cost_estimate=cost(1),
    )(
        tracers, kdiff, photolysis, u_wind, v_wind, day_count, day_order,
        polar, inner1, inner2, north_row, h_north, h_south, h_east, h_west,
    )


def solution(mesh):
    return jax.shard_map(
        body,
        mesh=mesh,
        in_specs=(
            P(None, "lon", "lat", None),
            P("lon", "lat", None),
            P("lon", "lat", None),
            P("lon", "lat", None),
            P("lon", "lat", None),
            P(),
            P("lon", "lat", None),
        ),
        out_specs=P(None, "lon", "lat", None),
        check_vma=False,
    )
```

```python
import jax
import jax.numpy as jnp
import numpy as np
from jax import lax
from jax.experimental import pallas as pl
from jax.experimental.pallas import tpu as pltpu
from jax.sharding import PartitionSpec as P

SECTIONS = 12
LEV = 128
UNROLL = 32
TURNS = LEV // UNROLL
PAIRS = SECTIONS // 2 - 1
F32 = jnp.float32
ANY = pl.BlockSpec(memory_space=pl.ANY)
SMEM = pl.BlockSpec(memory_space=pltpu.SMEM)
MESH = pl.DeviceIdType.MESH


def section_table(sections):
    bvals = [1.0 / 3.0] * 3 + [
        (j * j + j - 2.0) / (2.0 * j * (j + 1.0)) for j in range(3, sections + 1)
    ]
    scale = 4.0 / (sections * sections + sections - 2.0)
    lead = [1.0, 1.0]
    for j in range(2, sections + 1):
        lead.append(lead[-1] * (2.0 * j - 1.0) / j)
    rows = []
    for j in range(1, sections + 1):
        keep, share = 1.0 - bvals[j - 1], bvals[j - 1]
        shift = keep / (share * lead[j - 1])
        product = scale * share * lead[j - 1] / 2.0
        back = (j - 1.0) / j * lead[j - 2] / lead[j] if j > 1 else 0.0
        rows.append((shift, product, scale * shift / 2.0, back))
    return scale, 1.0 - bvals[sections], bvals[sections] * lead[sections], rows


SCALE, KEEP, SHARE, TABLE = section_table(SECTIONS)


def level_rows(level):
    return pl.ds(pl.multiple_of(level * 8, 8), 8)


def sixth(n):
    return lax.shift_right_logical(n * 10923, 16)


def sweep(cur, columns, finish, titration_of, side):
    def step(i, carry):
        here, below = list(carry[:4]), list(carry[4:])
        side(i)
        for r in range(UNROLL):
            level = i * UNROLL + r
            rows, above_rows = level_rows(level), level_rows(level + 1)
            mixing = columns[4, rows, :]
            above = [cur[q, above_rows, :] for q in range(4)]
            upward = [mixing * (above[q] - here[q]) for q in range(4)]
            state = [(here[q] + upward[q]) - below[q] for q in range(4)]
            titration = titration_of(rows, here)
            split = columns[5, rows, :] * here[3]
            net = split - titration
            joined = (0.75 * SCALE) * here[1] - columns[6, rows, :] * here[0]
            finish(
                rows,
                here,
                [
                    state[0] + (joined - titration),
                    state[1] + (split - joined),
                    state[2] + net,
                    state[3] - net,
                ],
            )
            here, below = above, upward
        return (*here, *below)

    zero = jnp.zeros((8, LEV), F32)
    init = tuple(cur[q, pl.ds(0, 8), :] for q in range(4)) + (zero,) * 4
    lax.fori_loop(0, TURNS, step, init)


def store_all(ref, rows, values):
    for q in range(4):
        ref[q, rows, :] = values[q]


def day_steps(columns, work, lit, table, side, after_first=None, after_pairs=None, after_turn=None):
    ping, pong, tit, final = work
    columns[4, pl.ds(LEV * 8 - 8, 8), :] = jnp.zeros((8, LEV), F32)

    def first_titration(rows, here):
        product = here[0] * here[2]
        tit[rows, :] = product
        return (SCALE / 2.0) * product

    def first_finish(rows, here, state):
        store_all(ping, rows, state)
        store_all(pong, rows, here)

    sweep(columns, columns, first_finish, first_titration, lambda i: side(i, True))
    if after_first is not None:
        after_first()

    def titration_with(shift, product, offset):
        def titration(rows, here):
            ozone = here[0] + shift * columns[0, rows, :]
            nitric = here[2] + shift * columns[2, rows, :]
            return product * ozone * nitric - offset * tit[rows, :]

        return titration

    def middle(pair, half, cur, out):
        section = 1 + 2 * pair + half
        shift, product, offset, back = [table[section, c] for c in range(4)]

        def finish(rows, here, state):
            store_all(out, rows, [state[q] - back * out[q, rows, :] for q in range(4)])

        base = TURNS * (1 + 2 * pair + half)
        sweep(cur, columns, finish, titration_with(shift, product, offset), lambda i: side(base + i, False))

    def both(pair, carry):
        middle(pair, 0, ping, pong)
        middle(pair, 1, pong, ping)
        return carry

    lax.fori_loop(0, PAIRS, both, 0)
    if after_pairs is not None:
        after_pairs()
    shift, product, offset, back = TABLE[SECTIONS - 1]

    def last_finish(rows, here, state):
        start = [columns[q, rows, :] for q in range(4)]
        half = 0.5 * tit[rows, :]
        gain = 0.75 * start[1]
        night = [start[0] + (gain - half), start[1] - gain, start[2] - half, start[3] + half]
        for q in range(4):
            day = SHARE * (state[q] - back * pong[q, rows, :]) + KEEP * start[q]
            final[q, rows, :] = jnp.where(lit, day, night[q])

    base = TURNS * (SECTIONS - 1)
    sweep(ping, columns, last_finish, titration_with(shift, product, offset), lambda i: side(base + i, False))


def tile_in(nat, row0, columns, tile, plane):
    src = pl.ds(pl.multiple_of(row0 + tile * 128, 8), 128)
    dst = pl.ds(tile, 128, stride=8)
    factor = jnp.where(plane >= 4, SCALE, 1.0).astype(F32)
    turned = (factor * nat[plane, src, :]).T
    columns[plane, dst, :] = turned
    columns[6, dst, :] = 0.125 * turned


def tile_in_turn(nat, row0, columns, turn):
    tile = sixth(turn)
    tile_in(nat, row0, columns, tile, turn - 6 * tile)


def tile_in_all(nat, row0, columns, ready):
    turn = 0
    for tiles, wait in ready:
        wait()

        def step(tile, carry):
            for plane in range(6):
                tile_in(nat, row0, columns, tile, jnp.int32(plane))
            return carry

        lax.fori_loop(turn, turn + tiles, step, 0)
        turn += tiles


def tile_out(final, put, tile, q):
    put(tile, q, final[q, pl.ds(tile, 128, stride=8), :].T)


def tile_out_turn(final, put, turn, is_first):
    if is_first:
        tile_out(final, put, 0, turn)
    else:
        job = jnp.minimum(turn - TURNS, 27)
        tile_out(final, put, 1 + lax.shift_right_logical(job, 2), lax.bitwise_and(job, 3))


def lit_bits(count_ref, order_ref):
    count = count_ref[lax.axis_index("lat"), lax.axis_index("lon")]

    def mark(i, bits):
        bit = lax.shift_left(jnp.int32(1), order_ref[0, 0, i])
        return lax.bitwise_or(bits, jnp.where(i < count, bit, 0))

    return lax.fori_loop(0, 32, mark, jnp.int32(0))


def lit_columns(bits, longitude_of):
    tile = lax.broadcasted_iota(jnp.int32, (8, LEV), 0)
    lane = lax.broadcasted_iota(jnp.int32, (8, LEV), 1)
    octet = tile * 16 + lax.shift_right_logical(lane, 3)
    block = lax.shift_right_logical(longitude_of(octet), 1)
    return lax.bitwise_and(lax.shift_right_logical(jnp.full((8, LEV), bits, jnp.int32), block), 1) > 0


def inner_longitude(octet):
    place = sixth(octet)
    return jnp.where(place == 0, 0, jnp.where(place == 1, 63, place - 1))


class Copies:
    def __init__(self, sems):
        self.sems, self.used = sems, 0

    def start(self, pairs):
        group = []
        for src, dst in pairs:
            copy = pltpu.make_async_copy(src, dst, self.sems.at[self.used])
            self.used += 1
            copy.start()
            group.append(copy)
        return lambda: [copy.wait() for copy in group]


def flat(ref):
    return ref.reshape(*ref.shape[:-3], ref.shape[-3] * ref.shape[-2], LEV)


def planes(y, k, p, nat, lons, lats, to_lons, to_rows):
    return [
        (y.at[:, lons, lats], nat.at[pl.ds(0, 4), to_lons, to_rows]),
        (k.at[lons, lats], nat.at[4, to_lons, to_rows]),
        (p.at[lons, lats], nat.at[5, to_lons, to_rows]),
    ]


def clear_pads(*refs):
    for ref in refs:
        for q in range(4):
            ref[q, pl.ds(LEV * 8, 8), :] = jnp.zeros((8, LEV), F32)


ROWS48, ALL48 = pl.ds(8, 48), pl.ds(0, 48)


def edge_kernel(
    y, k, p, u, v, count, order, table,
    polar, inner1, turned, h_north, h_south, h_east, h_west,
    nat1, nat2, nat3, cols_a, cols_b, ping, pong, tit, final, to_south, to_north, to_west, to_east,
    send, recv, sems,
):
    lon, lat = lax.axis_index("lon"), lax.axis_index("lat")
    lons, lats = lax.axis_size("lon"), lax.axis_size("lat")
    west, east = lax.rem(lon + lons - 1, lons), lax.rem(lon + 1, lons)
    south, north = lax.rem(lat + lats - 1, lats), lax.rem(lat + 1, lats)
    barrier = pltpu.get_barrier_semaphore()
    for device in ({"lon": west}, {"lon": east}, {"lat": south}, {"lat": north}):
        pl.semaphore_signal(barrier, inc=1, device_id=device, device_id_type=MESH)

    copies = Copies(sems)
    ready = []
    for c in range(4):
        part = pl.ds(16 * c, 16)
        ready.append((2, copies.start(
            planes(y, k, p, nat1, part, pl.ds(0, 8), part, pl.ds(0, 8))
            + planes(y, k, p, nat1, part, pl.ds(56, 8), part, pl.ds(8, 8))
        )))
    second = copies.start(
        planes(y, k, p, nat2, pl.ds(0, 1), ROWS48, pl.ds(0, 1), ALL48)
        + planes(y, k, p, nat2, pl.ds(63, 1), ROWS48, pl.ds(1, 1), ALL48)
        + planes(y, k, p, nat2, pl.ds(1, 20), ROWS48, pl.ds(2, 20), ALL48)
    )
    third = copies.start(planes(y, k, p, nat3, pl.ds(20, 22), ROWS48, pl.ds(0, 22), ALL48))
    winds = copies.start([(u.at[63], to_east.at[4]), (v.at[:, 63], to_north.at[4])])
    bits = lit_bits(count, order)
    clear_pads(cols_a, cols_b, ping, pong)
    flat1, flat2, flat3 = flat(nat1), flat(nat2), flat(nat3)

    def put_in(nat):
        def put(tile, q, value):
            nat[q, pl.ds(pl.multiple_of(tile * 128, 8), 128), :] = value

        return put

    work = (ping, pong, tit, final)
    tile_in_all(flat1, 0, cols_a, ready)
    second()

    def side1(turn, is_first):
        tile_in_turn(flat2, 0, cols_b, turn)

    day_steps(cols_a, work, lit_columns(bits, lambda octet: lax.shift_right_logical(octet, 1)), table, side1)
    third()

    def side2(turn, is_first):
        tile_in_turn(flat3, 16, cols_a, turn)
        tile_out_turn(final, put_in(flat1), turn, is_first)

    staged = []

    def after_pairs2():
        staged.append(copies.start([
            (nat1.at[pl.ds(0, 4)], polar),
            (nat1.at[pl.ds(0, 4), :, 0], to_south),
            (nat1.at[pl.ds(0, 4), :, 15], to_north.at[pl.ds(0, 4)]),
            (nat1.at[pl.ds(0, 4), 0, pl.ds(0, 8)], to_west.at[:, pl.ds(0, 8)]),
            (nat1.at[pl.ds(0, 4), 0, pl.ds(8, 8)], to_west.at[:, pl.ds(56, 8)]),
            (nat1.at[pl.ds(0, 4), 63, pl.ds(0, 8)], to_east.at[pl.ds(0, 4), pl.ds(0, 8)]),
            (nat1.at[pl.ds(0, 4), 63, pl.ds(8, 8)], to_east.at[pl.ds(0, 4), pl.ds(56, 8)]),
        ]))

    def side2_last(turn, is_first):
        tile_in_turn(flat3, 16, cols_a, turn)

    def side2_all(turn, is_first):
        side2(turn, is_first) if (is_first or not staged) else side2_last(turn, is_first)

    day_steps(
        cols_b, work, lit_columns(bits, inner_longitude), table, side2_all, after_pairs=after_pairs2
    )
    staged[0]()
    winds()
    pl.semaphore_wait(barrier, 4)
    sends = []

    def send_to(index, src, dst, device):
        copy = pltpu.make_async_remote_copy(
            src_ref=src, dst_ref=dst, send_sem=send.at[index], recv_sem=recv.at[index],
            device_id=device, device_id_type=MESH,
        )
        copy.start()
        sends.append(copy)

    send_to(0, to_south, h_north, {"lat": south})
    send_to(1, to_north, h_south, {"lat": north})

    stored = []

    def side3(turn, is_first):
        if is_first or not stored:
            tile_out_turn(final, put_in(flat2), turn, is_first)

    def after_first3():
        copies.start([
            (nat2.at[pl.ds(0, 4), 0], to_west.at[:, pl.ds(8, 48)]),
            (nat2.at[pl.ds(0, 4), 1], to_east.at[pl.ds(0, 4), pl.ds(8, 48)]),
        ])()
        send_to(2, to_west, h_east, {"lon": west})
        send_to(3, to_east, h_west, {"lon": east})

    def after_pairs3():
        stored.append(copies.start([(nat2.at[pl.ds(0, 4)], inner1)]))

    day_steps(
        cols_a, work, lit_columns(bits, lambda octet: inner_longitude(octet + 128)), table, side3,
        after_first=after_first3, after_pairs=after_pairs3,
    )
    out = copies.start([(final, turned)])
    stored[0]()
    for copy in sends:
        copy.wait()
    out()


CHUNK = 4


def last_kernel(
    y, k, p, u, v, count, order, table, polar, inner1, turned, h_north, h_south, h_east, h_west,
    out,
    nat, cols, ping, pong, tit, final, before,
    mixed, uwind, vwind, first_row, s_halo, w_halo, south, eastward, northward, stage_out,
    out_sems, sems,
):
    copies = Copies(sems)
    ready = []
    for lon, span in ((0, 12), (12, 10)):
        part = pl.ds(lon, span)
        ready.append((4, copies.start(planes(y, k, p, nat, pl.ds(41 + lon, span), ROWS48, part, ALL48))))
    earlier = copies.start([(turned, before)])
    body = pl.ds(1, 64)
    lats = pl.ds(16, 48)
    filled = copies.start([
        (u, uwind),
        (v, vwind),
        (polar.at[:, :, 0], first_row),
        (h_south, s_halo),
        (h_west, w_halo),
        (h_north, mixed.at[:, body, 72]),
        (h_east, mixed.at[:, 65, pl.ds(8, 64)]),
        (polar.at[:, :, pl.ds(0, 8)], mixed.at[:, body, pl.ds(8, 8)]),
        (polar.at[:, :, pl.ds(8, 8)], mixed.at[:, body, pl.ds(64, 8)]),
        (inner1.at[:, 0], mixed.at[:, 1, lats]),
        (inner1.at[:, 1], mixed.at[:, 64, lats]),
        (inner1.at[:, pl.ds(2, 19)], mixed.at[:, pl.ds(2, 19), lats]),
        (inner1.at[:, 21, pl.ds(0, 16)], mixed.at[:, 21, pl.ds(16, 16)]),
    ])
    bits = lit_bits(count, order)
    clear_pads(cols, ping, pong)

    def put_from(octet0):
        def put(tile, q, value):
            for r in range(16):
                octet = octet0 + tile * 16 + r
                place = sixth(octet)
                dst = pl.ds(pl.multiple_of((octet - 6 * place) * 8 + 16, 8), 8)
                mixed[q, place, dst, :] = value[r * 8 : r * 8 + 8]

        return put

    tile_in_all(flat(nat), 32, cols, ready)
    earlier()

    def side(turn, is_first):
        tile_out_turn(before, put_from(128), turn, is_first)

    day_steps(
        cols, (ping, pong, tit, final),
        lit_columns(bits, lambda octet: sixth(octet + 256) - 1), table, side,
    )

    def finish_tile(tile, carry):
        for q in range(4):
            tile_out(final, put_from(256), tile, q)
        return carry

    lax.fori_loop(0, 8, finish_tile, 0)
    filled()

    @pl.when(lax.axis_index("lat") == lax.axis_size("lat") - 1)
    def _():
        def clear(i, carry):
            for q in range(4):
                mixed[q, i + 1, pl.ds(72, 1), :] = jnp.zeros((1, LEV), F32)
            return carry

        lax.fori_loop(0, 64, clear, 0)

    inside = jnp.where(lax.axis_index("lat") > 0, 1.0, 0.0).astype(F32)
    for m in range(8):
        rows = pl.ds(8 * m, 8)
        wind, gust = w_halo[4, rows, :], inside * s_halo[4, rows, :]
        for q in range(4):
            eastward[q, rows, :] = wind * jnp.where(
                wind > 0, w_halo[q, rows, :], mixed[q, 1, pl.ds(8 + 8 * m, 8), :]
            )
            south[q, rows, :] = gust * jnp.where(gust > 0, s_halo[q, rows, :], first_row[q, rows, :])

    def out_copy(chunk, slot):
        return pltpu.make_async_copy(
            stage_out.at[slot], out.at[:, pl.ds(chunk * CHUNK, CHUNK)], out_sems.at[slot]
        )

    def chunk_step(chunk, carry):
        slot = lax.rem(chunk, 2)

        @pl.when(chunk >= 2)
        def _():
            out_copy(chunk - 2, slot).wait()

        def lon_step(couple, inner_carry):
            for side_lon in range(2):
                lon = chunk * CHUNK + couple * 2 + side_lon
                for q in range(4):
                    northward[side_lon, q, pl.ds(7, 1), :] = south[q, pl.ds(lon, 1), :]
            lon = chunk * CHUNK + couple * 2
            for m in range(8):
                rows = pl.ds(8 * m, 8)
                here_rows, ahead_rows = pl.ds(8 + 8 * m, 8), pl.ds(9 + 8 * m, 8)
                west = [eastward[q, rows, :] for q in range(4)]
                here = [mixed[q, lon + 1, here_rows, :] for q in range(4)]
                for side_lon in range(2):
                    at = lon + side_lon
                    wind, gust = uwind[at, rows, :], vwind[at, rows, :]
                    wind_up, gust_up = wind > 0, gust > 0
                    for q in range(4):
                        beyond = mixed[q, at + 2, here_rows, :]
                        east = wind * jnp.where(wind_up, here[q], beyond)
                        north = gust * jnp.where(gust_up, here[q], mixed[q, at + 1, ahead_rows, :])
                        northward[side_lon, q, here_rows, :] = north
                        below = northward[side_lon, q, pl.ds(7 + 8 * m, 8), :]
                        stage_out[slot, q, couple * 2 + side_lon, rows, :] = (
                            here[q] - (east - west[q]) - (north - below)
                        )
                        west[q], here[q] = east, beyond
                for q in range(4):
                    eastward[q, rows, :] = west[q]
            return inner_carry

        lax.fori_loop(0, CHUNK // 2, lon_step, 0)
        out_copy(chunk, slot).start()
        return carry

    chunks = 64 // CHUNK
    lax.fori_loop(0, chunks, chunk_step, 0)
    for chunk in (chunks - 2, chunks - 1):
        out_copy(chunk, chunk % 2).wait()


def shape(*dims):
    return jax.ShapeDtypeStruct(dims, F32)


def vmem(*dims):
    return pltpu.VMEM(dims, F32)


COLUMNS = vmem(7, LEV * 8 + 8, LEV)
WORK = [
    vmem(4, LEV * 8 + 8, LEV),
    vmem(4, LEV * 8 + 8, LEV),
    vmem(LEV * 8, LEV),
    vmem(4, LEV * 8, LEV),
]
DMA = pltpu.SemaphoreType.DMA


def cost(groups):
    return pl.CostEstimate(
        flops=groups * 128 * 1024 * 540, bytes_accessed=groups * 5 * 2**20, transcendentals=0
    )


def body(tracers, kdiff, photolysis, u_wind, v_wind, day_count, day_order):
    inputs = (
        tracers, kdiff, photolysis, u_wind, v_wind, day_count.T, day_order,
        jnp.asarray(np.array(TABLE, np.float32)),
    )
    halos = (shape(4, 64, LEV), shape(5, 64, LEV), shape(4, 64, LEV), shape(5, 64, LEV))
    parts = pl.pallas_call(
        edge_kernel,
        name="edge_groups",
        out_shape=(shape(4, 64, 16, LEV), shape(4, 22, 48, LEV), shape(4, LEV * 8, LEV), *halos),
        in_specs=[ANY] * 5 + [SMEM] * 3,
        out_specs=(ANY,) * 7,
        scratch_shapes=[
            vmem(6, 64, 16, LEV), vmem(6, 22, 48, LEV), vmem(6, 22, 48, LEV),
            COLUMNS, COLUMNS, *WORK,
            vmem(4, 64, LEV), vmem(5, 64, LEV), vmem(4, 64, LEV), vmem(5, 64, LEV),
            DMA((4,)), DMA((4,)), DMA((64,)),
        ],
        compiler_params=pltpu.CompilerParams(
            vmem_limit_bytes=60 * 2**20, collective_id=0, has_side_effects=True
        ),
        cost_estimate=cost(3),
    )(*inputs)

    return pl.pallas_call(
        last_kernel,
        name="last_group",
        out_shape=shape(4, 64, 64, LEV),
        in_specs=[ANY] * 5 + [SMEM] * 3 + [ANY] * 7,
        out_specs=ANY,
        scratch_shapes=[
            vmem(6, 22, 48, LEV), COLUMNS, *WORK, vmem(4, LEV * 8, LEV),
            vmem(4, 66, 80, LEV),
            vmem(64, 64, LEV),
            vmem(64, 64, LEV),
            vmem(4, 64, LEV),
            vmem(5, 64, LEV),
            vmem(5, 64, LEV),
            vmem(4, 64, LEV),
            vmem(4, 64, LEV),
            vmem(2, 4, 72, LEV),
            vmem(2, 4, CHUNK, 64, LEV),
            DMA((2,)), DMA((24,)),
        ],
        compiler_params=pltpu.CompilerParams(vmem_limit_bytes=60 * 2**20),
        cost_estimate=cost(1),
    )(*inputs, *parts)


def solution(mesh):
    return jax.shard_map(
        body,
        mesh=mesh,
        in_specs=(
            P(None, "lon", "lat", None),
            P("lon", "lat", None),
            P("lon", "lat", None),
            P("lon", "lat", None),
            P("lon", "lat", None),
            P(),
            P("lon", "lat", None),
        ),
        out_specs=P(None, "lon", "lat", None),
        check_vma=False,
    )
```

```python
import jax
import jax.numpy as jnp
import numpy as np
from jax import lax
from jax.experimental import pallas as pl
from jax.experimental.pallas import tpu as pltpu
from jax.sharding import PartitionSpec as P

SECTIONS = 12
LEV = 128
UNROLL = 32
TURNS = LEV // UNROLL
PAIRS = SECTIONS // 2 - 1
F32 = jnp.float32
ANY = pl.BlockSpec(memory_space=pl.ANY)
SMEM = pl.BlockSpec(memory_space=pltpu.SMEM)
MESH = pl.DeviceIdType.MESH


def section_table(sections):
    bvals = [1.0 / 3.0] * 3 + [
        (j * j + j - 2.0) / (2.0 * j * (j + 1.0)) for j in range(3, sections + 1)
    ]
    scale = 4.0 / (sections * sections + sections - 2.0)
    lead = [1.0, 1.0]
    for j in range(2, sections + 1):
        lead.append(lead[-1] * (2.0 * j - 1.0) / j)
    rows = []
    for j in range(1, sections + 1):
        keep, share = 1.0 - bvals[j - 1], bvals[j - 1]
        shift = keep / (share * lead[j - 1])
        product = scale * share * lead[j - 1] / 2.0
        back = (j - 1.0) / j * lead[j - 2] / lead[j] if j > 1 else 0.0
        rows.append((shift, product, scale * shift / 2.0, back))
    return scale, 1.0 - bvals[sections], bvals[sections] * lead[sections], rows


SCALE, KEEP, SHARE, TABLE = section_table(SECTIONS)


def level_rows(level):
    return pl.ds(pl.multiple_of(level * 8, 8), 8)


def sixth(n):
    return lax.shift_right_logical(n * 10923, 16)


def sweep(cur, columns, finish, titration_of, side, turn_end=None):
    def step(i, carry):
        here, below = list(carry[:4]), list(carry[4:])
        for r in range(UNROLL):
            if r == 8:
                side(i)
            level = i * UNROLL + r
            rows, above_rows = level_rows(level), level_rows(level + 1)
            mixing = columns[4, rows, :]
            above = [cur[q, above_rows, :] for q in range(4)]
            upward = [mixing * (above[q] - here[q]) for q in range(4)]
            state = [(here[q] + upward[q]) - below[q] for q in range(4)]
            titration = titration_of(rows, here)
            split = columns[5, rows, :] * here[3]
            net = split - titration
            joined = (0.75 * SCALE) * here[1] - columns[6, rows, :] * here[0]
            finish(
                rows,
                here,
                [
                    state[0] + (joined - titration),
                    state[1] + (split - joined),
                    state[2] + net,
                    state[3] - net,
                ],
            )
            here, below = above, upward
        if turn_end is not None:
            turn_end(i)
        return (*here, *below)

    zero = jnp.zeros((8, LEV), F32)
    init = tuple(cur[q, pl.ds(0, 8), :] for q in range(4)) + (zero,) * 4
    lax.fori_loop(0, TURNS, step, init)


def store_all(ref, rows, values):
    for q in range(4):
        ref[q, rows, :] = values[q]


def day_steps(columns, work, lit, table, side, after_first=None, after_pairs=None, turn_end=None):
    ping, pong, tit, final = work
    columns[4, pl.ds(LEV * 8 - 8, 8), :] = jnp.zeros((8, LEV), F32)

    def first_titration(rows, here):
        product = here[0] * here[2]
        tit[rows, :] = product
        return (SCALE / 2.0) * product

    def first_finish(rows, here, state):
        store_all(ping, rows, state)
        store_all(pong, rows, here)

    sweep(columns, columns, first_finish, first_titration, lambda i: side(i, "first"))
    if after_first is not None:
        after_first()

    def titration_with(shift, product, offset):
        def titration(rows, here):
            ozone = here[0] + shift * columns[0, rows, :]
            nitric = here[2] + shift * columns[2, rows, :]
            return product * ozone * nitric - offset * tit[rows, :]

        return titration

    def middle(pair, half, cur, out):
        section = 1 + 2 * pair + half
        shift, product, offset, back = [table[section, c] for c in range(4)]

        def finish(rows, here, state):
            store_all(out, rows, [state[q] - back * out[q, rows, :] for q in range(4)])

        base = TURNS * (1 + 2 * pair + half)
        sweep(cur, columns, finish, titration_with(shift, product, offset), lambda i: side(base + i, "middle"))

    def both(pair, carry):
        middle(pair, 0, ping, pong)
        middle(pair, 1, pong, ping)
        return carry

    lax.fori_loop(0, PAIRS, both, 0)
    if after_pairs is not None:
        after_pairs()
    shift, product, offset, back = TABLE[SECTIONS - 1]

    def last_finish(rows, here, state):
        start = [columns[q, rows, :] for q in range(4)]
        half = 0.5 * tit[rows, :]
        gain = 0.75 * start[1]
        night = [start[0] + (gain - half), start[1] - gain, start[2] - half, start[3] + half]
        for q in range(4):
            day = SHARE * (state[q] - back * pong[q, rows, :]) + KEEP * start[q]
            final[q, rows, :] = jnp.where(lit, day, night[q])

    base = TURNS * (SECTIONS - 1)
    sweep(ping, columns, last_finish, titration_with(shift, product, offset), lambda i: side(base + i, "last"), turn_end)


def tile_in(nat, row0, columns, tile, plane):
    src = pl.ds(pl.multiple_of(row0 + tile * 128, 8), 128)
    dst = pl.ds(tile, 128, stride=8)
    turned = nat[plane, src, :].T
    if isinstance(plane, int) and plane >= 4:
        turned = SCALE * turned
    columns[plane, dst, :] = turned
    if isinstance(plane, int) and plane == 5:
        columns[6, dst, :] = 0.125 * turned


def tile_in_turn(nat, row0, columns, turn, stage):
    if stage == "middle":
        job = jnp.minimum(turn - TURNS, 31)
        tile_in(nat, row0, columns, lax.shift_right_logical(job, 2), lax.bitwise_and(job, 3))
    else:
        plane, turn0 = (4, 0) if stage == "first" else (5, TURNS * (SECTIONS - 1))
        for half in range(2):
            tile_in(nat, row0, columns, 2 * (turn - turn0) + half, plane)


def tile_in_all(nat, row0, columns, ready):
    done = 0
    for tiles, wait in ready:
        wait()

        def step(tile, carry):
            for plane in range(6):
                tile_in(nat, row0, columns, tile, plane)
            return carry

        lax.fori_loop(done, done + tiles, step, 0)
        done += tiles


def tile_out(final, put, tile, q):
    put(tile, q, final[q, pl.ds(tile, 128, stride=8), :].T)


def tile_out_turn(final, put, turn, stage):
    if stage == "first":
        tile_out(final, put, 0, turn)
    elif stage == "middle":
        job = jnp.minimum(turn - TURNS, 27)
        tile_out(final, put, 1 + lax.shift_right_logical(job, 2), lax.bitwise_and(job, 3))


def lit_bits(count_ref, order_ref):
    count = count_ref[lax.axis_index("lat"), lax.axis_index("lon")]

    def mark(i, bits):
        bit = lax.shift_left(jnp.int32(1), order_ref[0, 0, i])
        return lax.bitwise_or(bits, jnp.where(i < count, bit, 0))

    return lax.fori_loop(0, 32, mark, jnp.int32(0))


def lit_columns(bits, longitude_of):
    tile = lax.broadcasted_iota(jnp.int32, (8, LEV), 0)
    lane = lax.broadcasted_iota(jnp.int32, (8, LEV), 1)
    octet = tile * 16 + lax.shift_right_logical(lane, 3)
    block = lax.shift_right_logical(longitude_of(octet), 1)
    return lax.bitwise_and(lax.shift_right_logical(jnp.full((8, LEV), bits, jnp.int32), block), 1) > 0


def inner_longitude(octet):
    place = sixth(octet)
    return jnp.where(place == 0, 0, jnp.where(place == 1, 63, place - 1))


class Copies:
    def __init__(self, sems):
        self.sems, self.used = sems, 0

    def start(self, pairs):
        group = []
        for src, dst in pairs:
            copy = pltpu.make_async_copy(src, dst, self.sems.at[self.used])
            self.used += 1
            copy.start()
            group.append(copy)
        return lambda: [copy.wait() for copy in group]


def flat(ref):
    return ref.reshape(*ref.shape[:-3], ref.shape[-3] * ref.shape[-2], LEV)


def planes(y, k, p, nat, lons, lats, to_lons, to_rows):
    return [
        (y.at[:, lons, lats], nat.at[pl.ds(0, 4), to_lons, to_rows]),
        (k.at[lons, lats], nat.at[4, to_lons, to_rows]),
        (p.at[lons, lats], nat.at[5, to_lons, to_rows]),
    ]


def clear_pads(*refs):
    for ref in refs:
        for q in range(4):
            ref[q, pl.ds(LEV * 8, 8), :] = jnp.zeros((8, LEV), F32)


ROWS48, ALL48 = pl.ds(8, 48), pl.ds(0, 48)


def day_kernel(
    y, k, p, u, v, count, order, table,
    polar, inner1, inner2, turned, h_north, h_south, h_east, h_west,
    nat1, nat2, nat3, nat4, cols_a, cols_b, ping, pong, tit, final, to_south, to_north, to_west, to_east,
    send, recv, turn_sems, sems,
):
    lon, lat = lax.axis_index("lon"), lax.axis_index("lat")
    lons, lats = lax.axis_size("lon"), lax.axis_size("lat")
    west, east = lax.rem(lon + lons - 1, lons), lax.rem(lon + 1, lons)
    south, north = lax.rem(lat + lats - 1, lats), lax.rem(lat + 1, lats)
    barrier = pltpu.get_barrier_semaphore()
    for device in ({"lon": west}, {"lon": east}, {"lat": south}, {"lat": north}):
        pl.semaphore_signal(barrier, inc=1, device_id=device, device_id_type=MESH)

    copies = Copies(sems)
    ready = []
    for c in range(4):
        part = pl.ds(16 * c, 16)
        ready.append((2, copies.start(
            planes(y, k, p, nat1, part, pl.ds(0, 8), part, pl.ds(0, 8))
            + planes(y, k, p, nat1, part, pl.ds(56, 8), part, pl.ds(8, 8))
        )))
    bits = lit_bits(count, order)
    clear_pads(cols_a, cols_b, ping, pong)
    flat1, flat2, flat3, flat4 = flat(nat1), flat(nat2), flat(nat3), flat(nat4)

    def put_in(nat, row0=0):
        def put(tile, q, value):
            nat[q, pl.ds(pl.multiple_of(row0 + tile * 128, 8), 128), :] = value

        return put

    work = (ping, pong, tit, final)
    later = []

    def second_part():
        ready[1][1]()
        later.append(copies.start(
            planes(y, k, p, nat2, pl.ds(0, 1), ROWS48, pl.ds(0, 1), ALL48)
            + planes(y, k, p, nat2, pl.ds(63, 1), ROWS48, pl.ds(1, 1), ALL48)
            + planes(y, k, p, nat2, pl.ds(1, 20), ROWS48, pl.ds(2, 20), ALL48)
        ))

    tile_in_all(flat1, 0, cols_a, [ready[0], (2, second_part), *ready[2:]])
    later[0]()
    third = copies.start(planes(y, k, p, nat3, pl.ds(20, 22), ROWS48, pl.ds(0, 22), ALL48))
    fourth = copies.start(planes(y, k, p, nat4, pl.ds(41, 22), ROWS48, pl.ds(0, 22), ALL48))
    winds = copies.start([(u.at[63], to_east.at[4]), (v.at[:, 63], to_north.at[4])])

    def side1(turn, stage):
        tile_in_turn(flat2, 0, cols_b, turn, stage)

    day_steps(cols_a, work, lit_columns(bits, lambda octet: lax.shift_right_logical(octet, 1)), table, side1)
    third()

    def side2(turn, stage):
        tile_in_turn(flat3, 16, cols_a, turn, stage)
        tile_out_turn(final, put_in(flat1), turn, stage)

    staged = []

    def after_pairs2():
        staged.append(copies.start([
            (nat1.at[pl.ds(0, 4)], polar),
            (nat1.at[pl.ds(0, 4), :, 0], to_south),
            (nat1.at[pl.ds(0, 4), :, 15], to_north.at[pl.ds(0, 4)]),
            (nat1.at[pl.ds(0, 4), 0, pl.ds(0, 8)], to_west.at[:, pl.ds(0, 8)]),
            (nat1.at[pl.ds(0, 4), 0, pl.ds(8, 8)], to_west.at[:, pl.ds(56, 8)]),
            (nat1.at[pl.ds(0, 4), 63, pl.ds(0, 8)], to_east.at[pl.ds(0, 4), pl.ds(0, 8)]),
            (nat1.at[pl.ds(0, 4), 63, pl.ds(8, 8)], to_east.at[pl.ds(0, 4), pl.ds(56, 8)]),
        ]))

    day_steps(
        cols_b, work, lit_columns(bits, inner_longitude), table, side2, after_pairs=after_pairs2
    )
    staged[0]()
    winds()
    pl.semaphore_wait(barrier, 4)
    sends = []

    def send_to(index, src, dst, device):
        copy = pltpu.make_async_remote_copy(
            src_ref=src, dst_ref=dst, send_sem=send.at[index], recv_sem=recv.at[index],
            device_id=device, device_id_type=MESH,
        )
        copy.start()
        sends.append(copy)

    send_to(0, to_south, h_north, {"lat": south})
    send_to(1, to_north, h_south, {"lat": north})

    stored = []

    fourth()

    def side3(turn, stage):
        tile_in_turn(flat4, 32, cols_b, turn, stage)
        tile_out_turn(final, put_in(flat2), turn, stage)

    def after_first3():
        copies.start([
            (nat2.at[pl.ds(0, 4), 0], to_west.at[:, pl.ds(8, 48)]),
            (nat2.at[pl.ds(0, 4), 1], to_east.at[pl.ds(0, 4), pl.ds(8, 48)]),
        ])()
        send_to(2, to_west, h_east, {"lon": west})
        send_to(3, to_east, h_west, {"lon": east})

    def turned_part(i):
        rows = pl.ds(pl.multiple_of(i * UNROLL * 8, 8), UNROLL * 8)
        return pltpu.make_async_copy(final.at[:, rows], turned.at[:, rows], turn_sems.at[i])

    def after_pairs3():
        stored.append(copies.start([(nat2.at[pl.ds(0, 4)], inner1)]))

    day_steps(
        cols_a, work, lit_columns(bits, lambda octet: inner_longitude(octet + 128)), table, side3,
        after_first=after_first3, after_pairs=after_pairs3,
    )

    def side4(turn, stage):
        tile_out_turn(final, put_in(flat3, 16), turn, stage)

    def after_pairs4():
        stored.append(copies.start([(nat3.at[pl.ds(0, 4)], inner2)]))

    day_steps(
        cols_b, work, lit_columns(bits, lambda octet: sixth(octet + 256) - 1), table, side4,
        after_pairs=after_pairs4, turn_end=lambda i: turned_part(i).start(),
    )
    stored[0]()
    stored[1]()
    for copy in sends:
        copy.wait()
    for i in range(TURNS):
        turned_part(i).wait()


CHUNK = 4


def transport_kernel(
    u, v, polar, inner1, inner2, turned, h_north, h_south, h_east, h_west,
    out,
    before, mixed, uwind, vwind, first_row, s_halo, w_halo, south, eastward, northward, stage_out,
    out_sems, sems,
):
    copies = Copies(sems)
    body = pl.ds(1, 64)
    lats = pl.ds(16, 48)
    earlier = copies.start([(turned, before)])
    filled = copies.start([
        (polar.at[:, :, 0], first_row),
        (h_south, s_halo),
        (h_west, w_halo),
        (h_north, mixed.at[:, body, 72]),
        (h_east, mixed.at[:, 65, pl.ds(8, 64)]),
        (polar.at[:, :, pl.ds(0, 8)], mixed.at[:, body, pl.ds(8, 8)]),
        (polar.at[:, :, pl.ds(8, 8)], mixed.at[:, body, pl.ds(64, 8)]),
        (inner1.at[:, 0], mixed.at[:, 1, lats]),
        (inner1.at[:, 1], mixed.at[:, 64, lats]),
        (inner1.at[:, pl.ds(2, 19)], mixed.at[:, pl.ds(2, 19), lats]),
        (inner1.at[:, 21, pl.ds(0, 16)], mixed.at[:, 21, pl.ds(16, 16)]),
        (inner2.at[:, 0, pl.ds(16, 32)], mixed.at[:, 21, pl.ds(32, 32)]),
        (inner2.at[:, pl.ds(1, 20)], mixed.at[:, pl.ds(22, 20), lats]),
        (inner2.at[:, 21, pl.ds(0, 32)], mixed.at[:, 42, pl.ds(16, 32)]),
        (u, uwind),
        (v, vwind),
    ])

    def put(tile, q, value):
        for r in range(16):
            octet = 256 + tile * 16 + r
            place = sixth(octet)
            dst = pl.ds(pl.multiple_of((octet - 6 * place) * 8 + 16, 8), 8)
            mixed[q, place, dst, :] = value[r * 8 : r * 8 + 8]

    earlier()

    def finish_tile(tile, carry):
        for q in range(4):
            tile_out(before, put, tile, q)
        return carry

    lax.fori_loop(0, 8, finish_tile, 0)
    filled()

    @pl.when(lax.axis_index("lat") == lax.axis_size("lat") - 1)
    def _():
        def clear(i, carry):
            for q in range(4):
                mixed[q, i + 1, pl.ds(72, 1), :] = jnp.zeros((1, LEV), F32)
            return carry

        lax.fori_loop(0, 64, clear, 0)

    inside = jnp.where(lax.axis_index("lat") > 0, 1.0, 0.0).astype(F32)
    for m in range(8):
        rows = pl.ds(8 * m, 8)
        wind, gust = w_halo[4, rows, :], inside * s_halo[4, rows, :]
        for q in range(4):
            eastward[q, rows, :] = wind * jnp.where(
                wind > 0, w_halo[q, rows, :], mixed[q, 1, pl.ds(8 + 8 * m, 8), :]
            )
            south[q, rows, :] = gust * jnp.where(gust > 0, s_halo[q, rows, :], first_row[q, rows, :])

    def out_copy(chunk):
        return pltpu.make_async_copy(
            stage_out.at[chunk], out.at[:, pl.ds(chunk * CHUNK, CHUNK)], out_sems.at[chunk]
        )

    def chunk_step(chunk, carry):
        def lon_step(couple, inner_carry):
            for side_lon in range(2):
                lon = chunk * CHUNK + couple * 2 + side_lon
                for q in range(4):
                    northward[side_lon, q, pl.ds(7, 1), :] = south[q, pl.ds(lon, 1), :]
            lon = chunk * CHUNK + couple * 2
            for m in range(8):
                rows = pl.ds(8 * m, 8)
                here_rows, ahead_rows = pl.ds(8 + 8 * m, 8), pl.ds(9 + 8 * m, 8)
                west = [eastward[q, rows, :] for q in range(4)]
                here = [mixed[q, lon + 1, here_rows, :] for q in range(4)]
                for side_lon in range(2):
                    at = lon + side_lon
                    wind, gust = uwind[at, rows, :], vwind[at, rows, :]
                    wind_up, gust_up = wind > 0, gust > 0
                    for q in range(4):
                        beyond = mixed[q, at + 2, here_rows, :]
                        east = wind * jnp.where(wind_up, here[q], beyond)
                        north = gust * jnp.where(gust_up, here[q], mixed[q, at + 1, ahead_rows, :])
                        northward[side_lon, q, here_rows, :] = north
                        below = northward[side_lon, q, pl.ds(7 + 8 * m, 8), :]
                        stage_out[chunk, q, couple * 2 + side_lon, rows, :] = (
                            here[q] - (east - west[q]) - (north - below)
                        )
                        west[q], here[q] = east, beyond
                for q in range(4):
                    eastward[q, rows, :] = west[q]
            return inner_carry

        lax.fori_loop(0, CHUNK // 2, lon_step, 0)
        out_copy(chunk).start()
        return carry

    lax.fori_loop(0, 64 // CHUNK, chunk_step, 0)

    def finish_chunk(chunk, carry):
        out_copy(chunk).wait()
        return carry

    lax.fori_loop(0, 64 // CHUNK, finish_chunk, 0)


def shape(*dims):
    return jax.ShapeDtypeStruct(dims, F32)


def vmem(*dims):
    return pltpu.VMEM(dims, F32)


COLUMNS = vmem(7, LEV * 8 + 8, LEV)
WORK = [
    vmem(4, LEV * 8 + 8, LEV),
    vmem(4, LEV * 8 + 8, LEV),
    vmem(LEV * 8, LEV),
    vmem(4, LEV * 8, LEV),
]
DMA = pltpu.SemaphoreType.DMA


def cost(groups):
    return pl.CostEstimate(
        flops=groups * 128 * 1024 * 540, bytes_accessed=groups * 5 * 2**20, transcendentals=0
    )


def body(tracers, kdiff, photolysis, u_wind, v_wind, day_count, day_order):
    inputs = (
        tracers, kdiff, photolysis, u_wind, v_wind, day_count.T, day_order,
        jnp.asarray(np.array(TABLE, np.float32)),
    )
    halos = (shape(4, 64, LEV), shape(5, 64, LEV), shape(4, 64, LEV), shape(5, 64, LEV))
    parts = pl.pallas_call(
        day_kernel,
        name="day_groups",
        out_shape=(
            shape(4, 64, 16, LEV), shape(4, 22, 48, LEV), shape(4, 22, 48, LEV), shape(4, LEV * 8, LEV),
            *halos,
        ),
        in_specs=[ANY] * 5 + [SMEM] * 3,
        out_specs=(ANY,) * 8,
        scratch_shapes=[
            vmem(6, 64, 16, LEV), vmem(6, 22, 48, LEV), vmem(6, 22, 48, LEV), vmem(6, 22, 48, LEV),
            COLUMNS, COLUMNS, *WORK,
            vmem(4, 64, LEV), vmem(5, 64, LEV), vmem(4, 64, LEV), vmem(5, 64, LEV),
            DMA((4,)), DMA((4,)), DMA((TURNS,)), DMA((64,)),
        ],
        compiler_params=pltpu.CompilerParams(
            vmem_limit_bytes=60 * 2**20, collective_id=0, has_side_effects=True
        ),
        cost_estimate=cost(4),
    )(*inputs)

    return pl.pallas_call(
        transport_kernel,
        name="transport",
        out_shape=shape(4, 64, 64, LEV),
        in_specs=[ANY] * 10,
        out_specs=ANY,
        scratch_shapes=[
            vmem(4, LEV * 8, LEV),
            vmem(4, 66, 80, LEV),
            vmem(64, 64, LEV),
            vmem(64, 64, LEV),
            vmem(4, 64, LEV),
            vmem(5, 64, LEV),
            vmem(5, 64, LEV),
            vmem(4, 64, LEV),
            vmem(4, 64, LEV),
            vmem(2, 4, 72, LEV),
            vmem(64 // CHUNK, 4, CHUNK, 64, LEV),
            DMA((64 // CHUNK,)), DMA((24,)),
        ],
        compiler_params=pltpu.CompilerParams(vmem_limit_bytes=60 * 2**20),
        cost_estimate=pl.CostEstimate(flops=2**21 * 10, bytes_accessed=20 * 2**20, transcendentals=0),
    )(u_wind, v_wind, *parts)


def solution(mesh):
    return jax.shard_map(
        body,
        mesh=mesh,
        in_specs=(
            P(None, "lon", "lat", None),
            P("lon", "lat", None),
            P("lon", "lat", None),
            P("lon", "lat", None),
            P("lon", "lat", None),
            P(),
            P("lon", "lat", None),
        ),
        out_specs=P(None, "lon", "lat", None),
        check_vma=False,
    )
```

```python
import jax
import jax.numpy as jnp
import numpy as np
from jax import lax
from jax.experimental import pallas as pl
from jax.experimental.pallas import tpu as pltpu
from jax.sharding import PartitionSpec as P

SECTIONS = 12
LEV = 128
UNROLL = 32
TURNS = LEV // UNROLL
PAIRS = SECTIONS // 2 - 1
F32 = jnp.float32
ANY = pl.BlockSpec(memory_space=pl.ANY)
SMEM = pl.BlockSpec(memory_space=pltpu.SMEM)
MESH = pl.DeviceIdType.MESH


def section_table(sections):
    bvals = [1.0 / 3.0] * 3 + [
        (j * j + j - 2.0) / (2.0 * j * (j + 1.0)) for j in range(3, sections + 1)
    ]
    scale = 4.0 / (sections * sections + sections - 2.0)
    lead = [1.0, 1.0]
    for j in range(2, sections + 1):
        lead.append(lead[-1] * (2.0 * j - 1.0) / j)
    rows = []
    for j in range(1, sections + 1):
        keep, share = 1.0 - bvals[j - 1], bvals[j - 1]
        shift = keep / (share * lead[j - 1])
        product = scale * share * lead[j - 1] / 2.0
        back = (j - 1.0) / j * lead[j - 2] / lead[j] if j > 1 else 0.0
        rows.append((shift, product, scale * shift / 2.0, back))
    return scale, 1.0 - bvals[sections], bvals[sections] * lead[sections], rows


SCALE, KEEP, SHARE, TABLE = section_table(SECTIONS)


def level_rows(level):
    return pl.ds(pl.multiple_of(level * 8, 8), 8)


def sixth(n):
    return lax.shift_right_logical(n * 10923, 16)


def sweep(cur, columns, finish, titration_of, side, turn_end=None):
    def step(i, carry):
        here, below = list(carry[:4]), list(carry[4:])
        for r in range(UNROLL):
            if r == 8:
                side(i)
            level = i * UNROLL + r
            rows, above_rows = level_rows(level), level_rows(level + 1)
            mixing = columns[4, rows, :]
            above = [cur[q, above_rows, :] for q in range(4)]
            upward = [mixing * (above[q] - here[q]) for q in range(4)]
            state = [(here[q] + upward[q]) - below[q] for q in range(4)]
            titration = titration_of(rows, here)
            split = columns[5, rows, :] * here[3]
            net = split - titration
            joined = (0.75 * SCALE) * here[1] - columns[6, rows, :] * here[0]
            finish(
                rows,
                here,
                [
                    state[0] + (joined - titration),
                    state[1] + (split - joined),
                    state[2] + net,
                    state[3] - net,
                ],
            )
            here, below = above, upward
        if turn_end is not None:
            turn_end(i)
        return (*here, *below)

    zero = jnp.zeros((8, LEV), F32)
    init = tuple(cur[q, pl.ds(0, 8), :] for q in range(4)) + (zero,) * 4
    lax.fori_loop(0, TURNS, step, init)


def store_all(ref, rows, values):
    for q in range(4):
        ref[q, rows, :] = values[q]


def day_steps(columns, work, lit, table, side, after_first=None, after_pairs=None, turn_end=None):
    ping, pong, tit, final = work
    columns[4, pl.ds(LEV * 8 - 8, 8), :] = jnp.zeros((8, LEV), F32)

    def first_titration(rows, here):
        product = here[0] * here[2]
        tit[rows, :] = product
        return (SCALE / 2.0) * product

    def first_finish(rows, here, state):
        store_all(ping, rows, state)
        store_all(pong, rows, here)

    sweep(columns, columns, first_finish, first_titration, lambda i: side(i, "first"))
    if after_first is not None:
        after_first()

    def titration_with(shift, product, offset):
        def titration(rows, here):
            ozone = here[0] + shift * columns[0, rows, :]
            nitric = here[2] + shift * columns[2, rows, :]
            return product * ozone * nitric - offset * tit[rows, :]

        return titration

    def middle(pair, half, cur, out, busy=True):
        section = 1 + 2 * pair + half
        shift, product, offset, back = [table[section, c] for c in range(4)]

        def finish(rows, here, state):
            store_all(out, rows, [state[q] - back * out[q, rows, :] for q in range(4)])

        base = TURNS * (1 + 2 * pair + half)
        sweep(cur, columns, finish, titration_with(shift, product, offset), lambda i: side(base + i, "middle") if busy else None)

    def both(pair, carry):
        middle(pair, 0, ping, pong)
        middle(pair, 1, pong, ping)
        return carry

    lax.fori_loop(0, PAIRS - 1, both, 0)
    if after_pairs is not None:
        after_pairs()
    middle(PAIRS - 1, 0, ping, pong, False)
    middle(PAIRS - 1, 1, pong, ping, False)
    shift, product, offset, back = TABLE[SECTIONS - 1]

    def last_finish(rows, here, state):
        start = [columns[q, rows, :] for q in range(4)]
        half = 0.5 * tit[rows, :]
        gain = 0.75 * start[1]
        night = [start[0] + (gain - half), start[1] - gain, start[2] - half, start[3] + half]
        for q in range(4):
            day = SHARE * (state[q] - back * pong[q, rows, :]) + KEEP * start[q]
            final[q, rows, :] = jnp.where(lit, day, night[q])

    base = TURNS * (SECTIONS - 1)
    sweep(ping, columns, last_finish, titration_with(shift, product, offset), lambda i: side(base + i, "last"), turn_end)


def tile_in(nat, row0, columns, tile, plane):
    src = pl.ds(pl.multiple_of(row0 + tile * 128, 8), 128)
    dst = pl.ds(tile, 128, stride=8)
    turned = nat[plane, src, :].T
    if isinstance(plane, int) and plane >= 4:
        turned = SCALE * turned
    columns[plane, dst, :] = turned
    if isinstance(plane, int) and plane == 5:
        columns[6, dst, :] = 0.125 * turned


def tile_in_turn(nat, row0, columns, turn, stage):
    if stage == "middle":
        job = turn - TURNS
        tile_in(nat, row0, columns, lax.shift_right_logical(job, 2), lax.bitwise_and(job, 3))
    else:
        plane, turn0 = (4, 0) if stage == "first" else (5, TURNS * (SECTIONS - 1))
        for half in range(2):
            tile_in(nat, row0, columns, 2 * (turn - turn0) + half, plane)


def tile_in_all(nat, row0, columns, ready):
    done = 0
    for tiles, wait in ready:
        wait()

        def step(tile, carry):
            for plane in range(6):
                tile_in(nat, row0, columns, tile, plane)
            return carry

        lax.fori_loop(done, done + tiles, step, 0)
        done += tiles


def tile_out(final, put, tile, q):
    put(tile, q, final[q, pl.ds(tile, 128, stride=8), :].T)


def tile_out_turn(final, put, turn, stage):
    if stage == "first":
        tile_out(final, put, 0, turn)
    elif stage == "middle":
        job = jnp.minimum(turn - TURNS, 27)
        tile_out(final, put, 1 + lax.shift_right_logical(job, 2), lax.bitwise_and(job, 3))


def lit_bits(count_ref, order_ref):
    count = count_ref[lax.axis_index("lat"), lax.axis_index("lon")]

    def mark(i, bits):
        bit = lax.shift_left(jnp.int32(1), order_ref[0, 0, i])
        return lax.bitwise_or(bits, jnp.where(i < count, bit, 0))

    return lax.fori_loop(0, 32, mark, jnp.int32(0))


def lit_columns(bits, longitude_of):
    tile = lax.broadcasted_iota(jnp.int32, (8, LEV), 0)
    lane = lax.broadcasted_iota(jnp.int32, (8, LEV), 1)
    octet = tile * 16 + lax.shift_right_logical(lane, 3)
    block = lax.shift_right_logical(longitude_of(octet), 1)
    return lax.bitwise_and(lax.shift_right_logical(jnp.full((8, LEV), bits, jnp.int32), block), 1) > 0


def inner_longitude(octet):
    place = sixth(octet)
    return jnp.where(place == 0, 0, jnp.where(place == 1, 63, place - 1))


class Copies:
    def __init__(self, sems):
        self.sems, self.used = sems, 0

    def start(self, pairs):
        group = []
        for src, dst in pairs:
            copy = pltpu.make_async_copy(src, dst, self.sems.at[self.used])
            self.used += 1
            copy.start()
            group.append(copy)
        return lambda: [copy.wait() for copy in group]


def flat(ref):
    return ref.reshape(*ref.shape[:-3], ref.shape[-3] * ref.shape[-2], LEV)


def planes(y, k, p, nat, lons, lats, to_lons, to_rows):
    return [
        (y.at[:, lons, lats], nat.at[pl.ds(0, 4), to_lons, to_rows]),
        (k.at[lons, lats], nat.at[4, to_lons, to_rows]),
        (p.at[lons, lats], nat.at[5, to_lons, to_rows]),
    ]


def clear_pads(*refs):
    for ref in refs:
        for q in range(4):
            ref[q, pl.ds(LEV * 8, 8), :] = jnp.zeros((8, LEV), F32)


ROWS48, ALL48 = pl.ds(8, 48), pl.ds(0, 48)


def day_kernel(
    y, k, p, u, v, count, order, table,
    polar, inner1, inner2, turned, h_north, h_south, h_east, h_west,
    nat1, nat2, nat3, nat4, cols_a, cols_b, ping, pong, tit, final, to_south, to_north, to_west, to_east,
    send, recv, turn_sems, sems,
):
    lon, lat = lax.axis_index("lon"), lax.axis_index("lat")
    lons, lats = lax.axis_size("lon"), lax.axis_size("lat")
    west, east = lax.rem(lon + lons - 1, lons), lax.rem(lon + 1, lons)
    south, north = lax.rem(lat + lats - 1, lats), lax.rem(lat + 1, lats)
    barrier = pltpu.get_barrier_semaphore()
    for device in ({"lon": west}, {"lon": east}, {"lat": south}, {"lat": north}):
        pl.semaphore_signal(barrier, inc=1, device_id=device, device_id_type=MESH)

    copies = Copies(sems)
    ready = []
    for c in range(4):
        part = pl.ds(16 * c, 16)
        ready.append((2, copies.start(
            planes(y, k, p, nat1, part, pl.ds(0, 8), part, pl.ds(0, 8))
            + planes(y, k, p, nat1, part, pl.ds(56, 8), part, pl.ds(8, 8))
        )))
    bits = lit_bits(count, order)
    clear_pads(cols_a, cols_b, ping, pong)
    flat1, flat2, flat3, flat4 = flat(nat1), flat(nat2), flat(nat3), flat(nat4)

    def put_in(nat, row0=0):
        def put(tile, q, value):
            nat[q, pl.ds(pl.multiple_of(row0 + tile * 128, 8), 128), :] = value

        return put

    work = (ping, pong, tit, final)
    later = []

    def second_part():
        ready[1][1]()
        later.append(copies.start(
            planes(y, k, p, nat2, pl.ds(0, 1), ROWS48, pl.ds(0, 1), ALL48)
            + planes(y, k, p, nat2, pl.ds(63, 1), ROWS48, pl.ds(1, 1), ALL48)
            + planes(y, k, p, nat2, pl.ds(1, 20), ROWS48, pl.ds(2, 20), ALL48)
        ))

    tile_in_all(flat1, 0, cols_a, [ready[0], (2, second_part), *ready[2:]])
    later[0]()
    third = copies.start(planes(y, k, p, nat3, pl.ds(20, 22), ROWS48, pl.ds(0, 22), ALL48))
    fourth = copies.start(planes(y, k, p, nat4, pl.ds(41, 22), ROWS48, pl.ds(0, 22), ALL48))
    winds = copies.start([(u.at[63], to_east.at[4]), (v.at[:, 63], to_north.at[4])])

    def side1(turn, stage):
        tile_in_turn(flat2, 0, cols_b, turn, stage)

    day_steps(cols_a, work, lit_columns(bits, lambda octet: lax.shift_right_logical(octet, 1)), table, side1)
    third()

    def side2(turn, stage):
        tile_in_turn(flat3, 16, cols_a, turn, stage)
        tile_out_turn(final, put_in(flat1), turn, stage)

    staged = []

    def after_pairs2():
        staged.append(copies.start([
            (nat1.at[pl.ds(0, 4)], polar),
            (nat1.at[pl.ds(0, 4), :, 0], to_south),
            (nat1.at[pl.ds(0, 4), :, 15], to_north.at[pl.ds(0, 4)]),
            (nat1.at[pl.ds(0, 4), 0, pl.ds(0, 8)], to_west.at[:, pl.ds(0, 8)]),
            (nat1.at[pl.ds(0, 4), 0, pl.ds(8, 8)], to_west.at[:, pl.ds(56, 8)]),
            (nat1.at[pl.ds(0, 4), 63, pl.ds(0, 8)], to_east.at[pl.ds(0, 4), pl.ds(0, 8)]),
            (nat1.at[pl.ds(0, 4), 63, pl.ds(8, 8)], to_east.at[pl.ds(0, 4), pl.ds(56, 8)]),
        ]))

    day_steps(
        cols_b, work, lit_columns(bits, inner_longitude), table, side2, after_pairs=after_pairs2
    )
    staged[0]()
    winds()
    pl.semaphore_wait(barrier, 4)
    sends = []

    def send_to(index, src, dst, device):
        copy = pltpu.make_async_remote_copy(
            src_ref=src, dst_ref=dst, send_sem=send.at[index], recv_sem=recv.at[index],
            device_id=device, device_id_type=MESH,
        )
        copy.start()
        sends.append(copy)

    send_to(0, to_south, h_north, {"lat": south})
    send_to(1, to_north, h_south, {"lat": north})

    stored = []

    fourth()

    def side3(turn, stage):
        tile_in_turn(flat4, 32, cols_b, turn, stage)
        tile_out_turn(final, put_in(flat2), turn, stage)

    def after_first3():
        copies.start([
            (nat2.at[pl.ds(0, 4), 0], to_west.at[:, pl.ds(8, 48)]),
            (nat2.at[pl.ds(0, 4), 1], to_east.at[pl.ds(0, 4), pl.ds(8, 48)]),
        ])()
        send_to(2, to_west, h_east, {"lon": west})
        send_to(3, to_east, h_west, {"lon": east})

    def turned_part(i):
        rows = pl.ds(pl.multiple_of(i * UNROLL * 8, 8), UNROLL * 8)
        return pltpu.make_async_copy(final.at[:, rows], turned.at[:, rows], turn_sems.at[i])

    def after_pairs3():
        stored.append(copies.start([(nat2.at[pl.ds(0, 4)], inner1)]))

    day_steps(
        cols_a, work, lit_columns(bits, lambda octet: inner_longitude(octet + 128)), table, side3,
        after_first=after_first3, after_pairs=after_pairs3,
    )

    def side4(turn, stage):
        tile_out_turn(final, put_in(flat3, 16), turn, stage)

    def after_pairs4():
        stored.append(copies.start([(nat3.at[pl.ds(0, 4)], inner2)]))

    day_steps(
        cols_b, work, lit_columns(bits, lambda octet: sixth(octet + 256) - 1), table, side4,
        after_pairs=after_pairs4, turn_end=lambda i: turned_part(i).start(),
    )
    stored[0]()
    stored[1]()
    for copy in sends:
        copy.wait()
    for i in range(TURNS):
        turned_part(i).wait()


CHUNK = 4


def transport_kernel(
    u, v, polar, inner1, inner2, turned, h_north, h_south, h_east, h_west,
    out,
    before, mixed, uwind, vwind, first_row, s_halo, w_halo, south, eastward, northward, stage_out,
    out_sems, sems,
):
    copies = Copies(sems)
    body = pl.ds(1, 64)
    lats = pl.ds(16, 48)

    def strips(lon, span):
        src, dst = pl.ds(lon, span), pl.ds(lon + 1, span)
        return [
            (polar.at[:, src, pl.ds(0, 8)], mixed.at[:, dst, pl.ds(8, 8)]),
            (polar.at[:, src, pl.ds(8, 8)], mixed.at[:, dst, pl.ds(64, 8)]),
        ]

    def winds(lon, span):
        lons = pl.ds(lon, span)
        return [(u.at[lons], uwind.at[lons]), (v.at[lons], vwind.at[lons])]

    west_part = copies.start([
        (polar.at[:, :, 0], first_row),
        (h_south, s_halo),
        (h_west, w_halo),
        (h_north, mixed.at[:, body, 72]),
        (h_east, mixed.at[:, 65, pl.ds(8, 64)]),
        *strips(0, 18),
        (inner1.at[:, 0], mixed.at[:, 1, lats]),
        (inner1.at[:, pl.ds(2, 19)], mixed.at[:, pl.ds(2, 19), lats]),
        (inner1.at[:, 21, pl.ds(0, 16)], mixed.at[:, 21, pl.ds(16, 16)]),
        *winds(0, 16),
    ])
    middle_part = copies.start([
        *strips(18, 24),
        (inner2.at[:, 0, pl.ds(16, 32)], mixed.at[:, 21, pl.ds(32, 32)]),
        (inner2.at[:, pl.ds(1, 20)], mixed.at[:, pl.ds(22, 20), lats]),
        (inner2.at[:, 21, pl.ds(0, 32)], mixed.at[:, 42, pl.ds(16, 32)]),
        *winds(16, 24),
    ])
    east_part = copies.start([
        (turned, before),
        *strips(42, 22),
        (inner1.at[:, 1], mixed.at[:, 64, lats]),
        *winds(40, 24),
    ])

    def put(tile, q, value):
        for r in range(16):
            octet = 256 + tile * 16 + r
            place = sixth(octet)
            dst = pl.ds(pl.multiple_of((octet - 6 * place) * 8 + 16, 8), 8)
            mixed[q, place, dst, :] = value[r * 8 : r * 8 + 8]

    def finish_tile(tile, carry):
        for q in range(4):
            tile_out(before, put, tile, q)
        return carry

    west_part()

    @pl.when(lax.axis_index("lat") == lax.axis_size("lat") - 1)
    def _():
        def clear(i, carry):
            for q in range(4):
                mixed[q, i + 1, pl.ds(72, 1), :] = jnp.zeros((1, LEV), F32)
            return carry

        lax.fori_loop(0, 64, clear, 0)

    inside = jnp.where(lax.axis_index("lat") > 0, 1.0, 0.0).astype(F32)
    for m in range(8):
        rows = pl.ds(8 * m, 8)
        wind, gust = w_halo[4, rows, :], inside * s_halo[4, rows, :]
        for q in range(4):
            eastward[q, rows, :] = wind * jnp.where(
                wind > 0, w_halo[q, rows, :], mixed[q, 1, pl.ds(8 + 8 * m, 8), :]
            )
            south[q, rows, :] = gust * jnp.where(gust > 0, s_halo[q, rows, :], first_row[q, rows, :])

    def out_copy(chunk):
        return pltpu.make_async_copy(
            stage_out.at[chunk], out.at[:, pl.ds(chunk * CHUNK, CHUNK)], out_sems.at[chunk]
        )

    def chunk_step(chunk, carry):
        def lon_step(couple, inner_carry):
            for side_lon in range(2):
                lon = chunk * CHUNK + couple * 2 + side_lon
                for q in range(4):
                    northward[side_lon, q, pl.ds(7, 1), :] = south[q, pl.ds(lon, 1), :]
            lon = chunk * CHUNK + couple * 2
            for m in range(8):
                rows = pl.ds(8 * m, 8)
                here_rows, ahead_rows = pl.ds(8 + 8 * m, 8), pl.ds(9 + 8 * m, 8)
                west = [eastward[q, rows, :] for q in range(4)]
                here = [mixed[q, lon + 1, here_rows, :] for q in range(4)]
                for side_lon in range(2):
                    at = lon + side_lon
                    wind, gust = uwind[at, rows, :], vwind[at, rows, :]
                    wind_up, gust_up = wind > 0, gust > 0
                    for q in range(4):
                        beyond = mixed[q, at + 2, here_rows, :]
                        east = wind * jnp.where(wind_up, here[q], beyond)
                        north = gust * jnp.where(gust_up, here[q], mixed[q, at + 1, ahead_rows, :])
                        northward[side_lon, q, here_rows, :] = north
                        below = northward[side_lon, q, pl.ds(7 + 8 * m, 8), :]
                        stage_out[chunk, q, couple * 2 + side_lon, rows, :] = (
                            here[q] - (east - west[q]) - (north - below)
                        )
                        west[q], here[q] = east, beyond
                for q in range(4):
                    eastward[q, rows, :] = west[q]
            return inner_carry

        lax.fori_loop(0, CHUNK // 2, lon_step, 0)
        out_copy(chunk).start()
        return carry

    lax.fori_loop(0, 16 // CHUNK, chunk_step, 0)
    middle_part()
    lax.fori_loop(16 // CHUNK, 40 // CHUNK, chunk_step, 0)
    east_part()
    lax.fori_loop(0, 8, finish_tile, 0)
    lax.fori_loop(40 // CHUNK, 64 // CHUNK, chunk_step, 0)

    def finish_chunk(chunk, carry):
        out_copy(chunk).wait()
        return carry

    lax.fori_loop(0, 64 // CHUNK, finish_chunk, 0)


def shape(*dims):
    return jax.ShapeDtypeStruct(dims, F32)


def vmem(*dims):
    return pltpu.VMEM(dims, F32)


COLUMNS = vmem(7, LEV * 8 + 8, LEV)
WORK = [
    vmem(4, LEV * 8 + 8, LEV),
    vmem(4, LEV * 8 + 8, LEV),
    vmem(LEV * 8, LEV),
    vmem(4, LEV * 8, LEV),
]
DMA = pltpu.SemaphoreType.DMA


def cost(groups):
    return pl.CostEstimate(
        flops=groups * 128 * 1024 * 540, bytes_accessed=groups * 5 * 2**20, transcendentals=0
    )


def body(tracers, kdiff, photolysis, u_wind, v_wind, day_count, day_order):
    inputs = (
        tracers, kdiff, photolysis, u_wind, v_wind, day_count.T, day_order,
        jnp.asarray(np.array(TABLE, np.float32)),
    )
    halos = (shape(4, 64, LEV), shape(5, 64, LEV), shape(4, 64, LEV), shape(5, 64, LEV))
    parts = pl.pallas_call(
        day_kernel,
        name="day_groups",
        out_shape=(
            shape(4, 64, 16, LEV), shape(4, 22, 48, LEV), shape(4, 22, 48, LEV), shape(4, LEV * 8, LEV),
            *halos,
        ),
        in_specs=[ANY] * 5 + [SMEM] * 3,
        out_specs=(ANY,) * 8,
        scratch_shapes=[
            vmem(6, 64, 16, LEV), vmem(6, 22, 48, LEV), vmem(6, 22, 48, LEV), vmem(6, 22, 48, LEV),
            COLUMNS, COLUMNS, *WORK,
            vmem(4, 64, LEV), vmem(5, 64, LEV), vmem(4, 64, LEV), vmem(5, 64, LEV),
            DMA((4,)), DMA((4,)), DMA((TURNS,)), DMA((64,)),
        ],
        compiler_params=pltpu.CompilerParams(
            vmem_limit_bytes=60 * 2**20, collective_id=0, has_side_effects=True
        ),
        cost_estimate=cost(4),
    )(*inputs)

    return pl.pallas_call(
        transport_kernel,
        name="transport",
        out_shape=shape(4, 64, 64, LEV),
        in_specs=[ANY] * 10,
        out_specs=ANY,
        scratch_shapes=[
            vmem(4, LEV * 8, LEV),
            vmem(4, 66, 80, LEV),
            vmem(64, 64, LEV),
            vmem(64, 64, LEV),
            vmem(4, 64, LEV),
            vmem(5, 64, LEV),
            vmem(5, 64, LEV),
            vmem(4, 64, LEV),
            vmem(4, 64, LEV),
            vmem(2, 4, 72, LEV),
            vmem(64 // CHUNK, 4, CHUNK, 64, LEV),
            DMA((64 // CHUNK,)), DMA((32,)),
        ],
        compiler_params=pltpu.CompilerParams(vmem_limit_bytes=60 * 2**20),
        cost_estimate=pl.CostEstimate(flops=2**21 * 10, bytes_accessed=20 * 2**20, transcendentals=0),
    )(u_wind, v_wind, *parts)


def solution(mesh):
    return jax.shard_map(
        body,
        mesh=mesh,
        in_specs=(
            P(None, "lon", "lat", None),
            P("lon", "lat", None),
            P("lon", "lat", None),
            P("lon", "lat", None),
            P("lon", "lat", None),
            P(),
            P("lon", "lat", None),
        ),
        out_specs=P(None, "lon", "lat", None),
        check_vma=False,
    )
```
